32 devices in a mesh: parts: 2 (over y), clus: 4 (over z), mem: 2 (over x), sub: 2 (over core).
Axes of the slice: x: 2, y: 2, z: 4, core: 2. Of those that a mesh axis runs over, the one named last changes fastest.
Arguments:
- embeddings: bfloat16 [4096, 1024], P(('parts', 'clus', 'mem', 'sub')), parts along dimension 0, as said below
- labels: int32 [4096], P(('parts', 'clus', 'mem', 'sub')), parts along dimension 0, may hold values from 0 to 15, as said below
- member_rank: int32 [4096], P(('parts', 'clus', 'mem', 'sub')), parts along dimension 0, may hold values from 0 to 2047, each once
Outputs:
- nearest: float32 [4096], P(('parts', 'clus', 'mem', 'sub')), parts along dimension 0
The draws below stay inside these ranges and needn't reach their ends.
There are 2 independent parts, one for each index of `parts`. The reference program is written for one: setup_inputs(seed, part) draws one part's arguments, and reference() takes and returns one part's arrays. A program takes and returns all parts, laid end to end along the dimension named above; each array names one. Nothing has to cross between parts.
Inputs may be any that keep to these rules, and one draw needn't show every extreme that they name: `embeddings`: each row has unit length up to rounding. Among the rows of one device, at most 32 have labels in any one group of 2 consecutive clusters (label // 2); on every device some group has exactly 32.
All inputs are finite; a program needn't handle non-finite values.
Results may differ from the reference program's by a relative error of at most 0.0003.
Values may be sent and summed in bfloat16 or wider, within the bound.
A program may use at most 64 MiB of HBM per device.

```python
import jax
import jax.numpy as jnp
from jax import lax

D = 1024
ROWS_DEV = 128
CLUS_GROUP = 2
GROUPS = 8
CAPACITY = 32
SLOTS = 256
SHARDS = 16
MEMBERS = 2048
CLUSTERS = 16


def member_layout(key):
    base = jax.random.fold_in(key, 11)
    key_full, key_score, key_shuffle, key_first, key_second = jax.random.split(base, 5)
    full_group = jax.random.randint(key_full, (SHARDS,), 0, GROUPS)
    scores = jax.random.randint(key_score, (SHARDS, SLOTS), 0, 1 << 20)
    slot_group = jnp.arange(SLOTS, dtype=jnp.int32) // CAPACITY
    scores = jnp.where(slot_group[None, :] == full_group[:, None], -1, scores)
    chosen = jnp.argsort(scores, axis=1, stable=True)[:, :ROWS_DEV].astype(jnp.int32)
    shuffle_key = jax.random.randint(key_shuffle, (SHARDS, ROWS_DEV), 0, 1 << 20)
    shuffle_order = jnp.argsort(shuffle_key, axis=1, stable=True)
    chosen = jnp.take_along_axis(chosen, shuffle_order, axis=1)
    within = jnp.minimum(jax.random.randint(key_first, (SHARDS, ROWS_DEV), 0, CLUS_GROUP), jax.random.randint(key_second, (SHARDS, ROWS_DEV), 0, CLUS_GROUP))
    label_all = chosen // CAPACITY * CLUS_GROUP + within
    return label_all.reshape(-1).astype(jnp.int32)


def draw_labels(key, part):
    return member_layout(key)


def draw_embeddings(key, part):
    label_all = member_layout(key)
    key_centre, key_weight, key_noise = jax.random.split(jax.random.fold_in(key, 23), 3)
    centre = jax.random.normal(key_centre, (CLUSTERS, D), jnp.float32)
    centre = centre / jnp.sqrt(jnp.sum(centre * centre, axis=1, keepdims=True))
    weight = jax.random.uniform(key_weight, (MEMBERS, 1), jnp.float32, 0.2, 0.95)
    noise_vec = jax.random.normal(key_noise, (MEMBERS, D), jnp.float32)
    noise_vec = noise_vec / jnp.sqrt(jnp.sum(noise_vec * noise_vec, axis=1, keepdims=True))
    mixed_vec = weight * centre[label_all] + jnp.sqrt(1.0 - weight * weight) * noise_vec
    mixed_vec = mixed_vec / jnp.sqrt(jnp.sum(mixed_vec * mixed_vec, axis=1, keepdims=True))
    return mixed_vec.astype(jnp.bfloat16)


def setup_inputs(seed: int = 0, part: int = 0) -> dict:
    key_list = jax.random.split(jax.random.key(seed), 4)
    own_keys = jax.random.split(jax.random.fold_in(key_list[3], part), 4)
    embeddings = draw_embeddings(jax.random.fold_in(jax.random.fold_in(key_list[3], part), 71), part)
    labels = draw_labels(jax.random.fold_in(jax.random.fold_in(key_list[3], part), 71), part)
    member_rank = jax.random.permutation(own_keys[2], MEMBERS).astype(jnp.int32)
    return dict(embeddings=embeddings, labels=labels, member_rank=member_rank)


def reference(embeddings, labels, member_rank):
    group_of = labels // CLUS_GROUP
    member_count = embeddings.shape[0]
    group_width = SHARDS * CAPACITY

    def per_group(group_id):
        in_group = group_of == group_id
        member_idx = jnp.nonzero(in_group, size=group_width, fill_value=0)[0].astype(jnp.int32)
        live_slot = jnp.arange(group_width) < jnp.sum(in_group)
        slot_emb = embeddings[member_idx]
        slot_label = jnp.where(live_slot, labels[member_idx], -1)
        slot_rank = member_rank[member_idx]
        scores = jnp.dot(slot_emb, slot_emb.T, preferred_element_type=jnp.float32)
        allowed = (slot_label[:, None] == slot_label[None, :]) & (slot_label[:, None] >= 0)
        allowed = allowed & (slot_rank[None, :] < slot_rank[:, None])
        nearest = jnp.max(jnp.where(allowed, scores, jnp.float32(-1.0)), axis=1)
        return jnp.where(live_slot, member_idx, member_count), nearest

    all_idx, all_best = lax.map(per_group, jnp.arange(GROUPS, dtype=jnp.int32))
    result = jnp.full((member_count,), -1.0, jnp.float32)
    return result.at[all_idx.reshape(-1)].set(all_best.reshape(-1), mode="drop")
```

```python
import functools
import math

import jax
import jax.numpy as jnp
from jax import lax
from jax.experimental import pallas as pl
from jax.experimental.pallas import tpu as pltpu
from jax.sharding import PartitionSpec as P

CLUS_GROUP = 2
MESH = pl.DeviceIdType.MESH
ROW_TILE = 16
LANES = 128
BYTE = 256
CLASS_STEP = BYTE * BYTE


def flipped(index, mask, size):
    out = 0
    bit = 1
    while bit < size:
        digit = lax.rem(lax.div(index, bit), 2)
        out = out + ((1 - digit) if mask & bit else digit) * bit
        bit *= 2
    return out


def nt_dot(lhs, rhs):
    return lax.dot_general(lhs, rhs, (((1,), (1,)), ((), ())), preferred_element_type=jnp.float32)


def dedup_kernel(
    clus_count,
    mem_count,
    capacity,
    emb_hbm,
    label_ref,
    rank_ref,
    out_ref,
    emb,
    send,
    own,
    sib,
    key_out,
    key_in,
    key_own,
    key_sib,
    ret_out,
    ret_in,
    load_sem,
    emb_send,
    emb_recv,
    key_send,
    key_recv,
    fwd_send,
    fwd_recv,
    kf_send,
    kf_recv,
    ret_send,
    ret_recv,
):
    groups = clus_count * mem_count
    rows = emb.shape[0]
    slots = groups * capacity
    tiles = slots // LANES
    per_tile = LANES // capacity
    clus = lax.axis_index("clus")
    mem = lax.axis_index("mem")
    sub = lax.axis_index("sub")
    me = clus * mem_count + mem

    load = pltpu.make_async_copy(emb_hbm, emb, load_sem)
    load.start()

    def partner(k):
        return {
            "clus": flipped(clus, k // mem_count, clus_count),
            "mem": flipped(mem, k % mem_count, mem_count),
        }

    sibling = {"sub": 1 - sub}
    far_first = list(range(groups - 1, 0, -1))
    barrier = pltpu.get_barrier_semaphore()
    for k in far_first:
        pl.semaphore_signal(barrier, inc=1, device_id=partner(k), device_id_type=MESH)
    pl.semaphore_signal(barrier, inc=1, device_id=sibling, device_id_type=MESH)

    labels = label_ref[...]
    group = lax.div(labels, CLUS_GROUP)
    relative = jnp.bitwise_xor(group, me)
    group_iota = lax.broadcasted_iota(jnp.int32, (groups, rows), 0)
    member = group_iota == relative
    before = lax.broadcasted_iota(jnp.int32, (rows, rows), 0) < lax.broadcasted_iota(
        jnp.int32, (rows, rows), 1
    )
    counts = jnp.dot(
        member.astype(jnp.float32).astype(jnp.bfloat16),
        before.astype(jnp.float32).astype(jnp.bfloat16),
        preferred_element_type=jnp.float32,
    )
    slot = jnp.sum(
        jnp.where(member, counts + (group_iota * capacity).astype(jnp.float32), 0.0),
        axis=0,
        keepdims=True,
    ).astype(jnp.int32)
    place = (
        (lax.broadcasted_iota(jnp.int32, (slots, rows), 0) == slot)
        .astype(jnp.float32)
        .astype(jnp.bfloat16)
    )

    ranks = rank_ref[...]
    row_iota = lax.broadcasted_iota(jnp.int32, (8, rows), 0)
    digits = jnp.where(
        row_iota == 0,
        labels - group * CLUS_GROUP + 1,
        jnp.where(
            row_iota == 1,
            lax.div(ranks, BYTE),
            jnp.where(row_iota == 2, lax.rem(ranks, BYTE), 0),
        ),
    )
    placed = nt_dot(digits.astype(jnp.float32).astype(jnp.bfloat16), place)
    keys = placed[0:1] * float(CLASS_STEP) + placed[1:2] * float(BYTE) + placed[2:3]
    for t in range(tiles):
        key_out[t] = keys[:, t * LANES : (t + 1) * LANES]

    load.wait()

    def fill(first, count):
        span = pl.ds(first * capacity, count * capacity)
        send[span, :] = jnp.dot(
            place[first * capacity : (first + count) * capacity],
            emb[...],
            preferred_element_type=jnp.float32,
        ).astype(jnp.bfloat16)

    def block(ref, k):
        return ref.at[pl.ds(k * capacity, capacity), :]

    emb_copies, key_copies = {}, {}
    for k in far_first:
        emb_copies[k] = pltpu.make_async_remote_copy(
            src_ref=block(send, k),
            dst_ref=block(own, k),
            send_sem=emb_send.at[k],
            recv_sem=emb_recv.at[k],
            device_id=partner(k),
            device_id_type=MESH,
        )
        key_copies[k] = pltpu.make_async_remote_copy(
            src_ref=key_out.at[k // per_tile],
            dst_ref=key_in.at[k],
            send_sem=key_send.at[k],
            recv_sem=key_recv.at[k],
            device_id=partner(k),
            device_id_type=MESH,
        )
    half = groups // 2
    fill(half, half)
    pl.semaphore_wait(barrier, groups)
    for k in far_first:
        key_copies[k].start()
    for k in far_first[:half]:
        emb_copies[k].start()
    fill(0, half)
    for k in far_first[half:]:
        emb_copies[k].start()
    own[pl.ds(0, capacity), :] = send[pl.ds(0, capacity), :]

    forwards = {}
    for k in range(groups):
        forwards[k] = pltpu.make_async_remote_copy(
            src_ref=block(send if k == 0 else own, k),
            dst_ref=block(sib, k),
            send_sem=fwd_send.at[k],
            recv_sem=fwd_recv.at[k],
            device_id=sibling,
            device_id_type=MESH,
        )
    forwards[0].start()
    lane_block = lax.div(lax.broadcasted_iota(jnp.int32, (1, LANES), 1), capacity)
    for k in range(1, groups):
        key_copies[k].wait_recv()
    for t in range(tiles):
        row = jnp.zeros((1, LANES), jnp.float32)
        for k in range(t * per_tile, (t + 1) * per_tile):
            piece = key_out[t] if k == 0 else key_in[k]
            row = jnp.where(lane_block == k % per_tile, piece, row)
        key_own[t] = row
    key_forward = pltpu.make_async_remote_copy(
        src_ref=key_own,
        dst_ref=key_sib,
        send_sem=kf_send,
        recv_sem=kf_recv,
        device_id=sibling,
        device_id_type=MESH,
    )
    key_forward.start()
    for k in range(1, groups):
        emb_copies[k].wait_recv()
        forwards[k].start()
    key_forward.wait_recv()

    row_keys = jnp.concatenate([key_own[t] for t in range(tiles)], axis=1)
    row_base = (
        lax.div(row_keys.astype(jnp.int32), CLASS_STEP) * CLASS_STEP
    ).astype(jnp.float32)
    row_base = jnp.maximum(row_base, 1.0)

    def masked(cands, cand_keys):
        scores = nt_dot(cands[...], own[...])
        best = jnp.full((1, slots), -1.0, jnp.float32)
        for t in range(tiles):
            column = jnp.transpose(jnp.broadcast_to(cand_keys[t], (LANES, LANES)))
            column = jnp.concatenate([column] * tiles, axis=1)
            allowed = (column < row_keys) & (column >= row_base)
            piece = jnp.where(allowed, scores[t * LANES : (t + 1) * LANES], -1.0)
            best = jnp.maximum(best, jnp.max(piece, axis=0, keepdims=True))
        return best

    best = masked(own, key_own)
    for k in range(groups):
        forwards[k].wait_recv()
    best = jnp.maximum(best, masked(sib, key_sib))
    for t in range(tiles):
        ret_out[t] = best[:, t * LANES : (t + 1) * LANES]

    returns = {}
    for k in far_first:
        returns[k] = pltpu.make_async_remote_copy(
            src_ref=ret_out.at[k // per_tile],
            dst_ref=ret_in.at[k],
            send_sem=ret_send.at[k],
            recv_sem=ret_recv.at[k],
            device_id=partner(k),
            device_id_type=MESH,
        )
        returns[k].start()
    for k in far_first:
        emb_copies[k].wait_send()
        key_copies[k].wait_send()
    for k in range(groups):
        forwards[k].wait_send()
    key_forward.wait_send()
    for k in range(1, groups):
        returns[k].wait_recv()

    pieces = []
    for t in range(tiles):
        row = jnp.zeros((1, LANES), jnp.float32)
        for k in range(t * per_tile, (t + 1) * per_tile):
            piece = ret_out[t] if k == 0 else ret_in[k]
            row = jnp.where(lane_block == k % per_tile, piece, row)
        pieces.append(row)
    result = jnp.concatenate(pieces, axis=1)
    high = result.astype(jnp.bfloat16).astype(jnp.float32)
    middle = (result - high).astype(jnp.bfloat16).astype(jnp.float32)
    low = result - high - middle
    split_iota = lax.broadcasted_iota(jnp.int32, (8, slots), 0)
    split = jnp.where(
        split_iota == 0,
        high,
        jnp.where(split_iota == 1, middle, jnp.where(split_iota == 2, low, 0.0)),
    ).astype(jnp.bfloat16)
    taken = jnp.dot(split, place, preferred_element_type=jnp.float32)
    out_ref[...] = taken[0:1] + taken[1:2] + taken[2:3]
    for k in far_first:
        returns[k].wait_send()


def kernel_body(clus_count, mem_count, embeddings, labels, member_rank):
    rows, width = embeddings.shape
    groups = clus_count * mem_count
    capacity = 2 * rows // groups
    slots = groups * capacity
    tiles = slots // LANES
    dma = pltpu.SemaphoreType.DMA
    vmem = pl.BlockSpec(memory_space=pltpu.VMEM)
    out = pl.pallas_call(
        functools.partial(dedup_kernel, clus_count, mem_count, capacity),
        out_shape=jax.ShapeDtypeStruct((1, rows), jnp.float32),
        in_specs=[pl.BlockSpec(memory_space=pl.ANY), vmem, vmem],
        out_specs=vmem,
        scratch_shapes=[
            pltpu.VMEM((rows, width), jnp.bfloat16),
            pltpu.VMEM((slots, width), jnp.bfloat16),
            pltpu.VMEM((slots, width), jnp.bfloat16),
            pltpu.VMEM((slots, width), jnp.bfloat16),
            pltpu.VMEM((tiles, 1, LANES), jnp.float32),
            pltpu.VMEM((groups, 1, LANES), jnp.float32),
            pltpu.VMEM((tiles, 1, LANES), jnp.float32),
            pltpu.VMEM((tiles, 1, LANES), jnp.float32),
            pltpu.VMEM((tiles, 1, LANES), jnp.float32),
            pltpu.VMEM((groups, 1, LANES), jnp.float32),
            dma,
            dma((groups,)),
            dma((groups,)),
            dma((groups,)),
            dma((groups,)),
            dma((groups,)),
            dma((groups,)),
            dma,
            dma,
            dma((groups,)),
            dma((groups,)),
        ],
        compiler_params=pltpu.CompilerParams(collective_id=0, has_side_effects=True),
    )(embeddings, labels.reshape(1, rows), member_rank.reshape(1, rows))
    return out.reshape(rows)


def fits_kernel(clus_count, mem_count, sub_count, rows):
    groups = clus_count * mem_count
    capacity = 2 * rows // groups
    return (
        clus_count & (clus_count - 1) == 0
        and mem_count & (mem_count - 1) == 0
        and sub_count == 2
        and groups >= 2
        and rows % LANES == 0
        and capacity % ROW_TILE == 0
        and LANES % capacity == 0
        and rows * groups * sub_count <= CLASS_STEP
    )


def swapped(value, axis, stride):
    mask = 2**stride
    pairs = [(source, source ^ mask) for source in range(lax.axis_size(axis))]
    return lax.ppermute(value, axis, pairs)


def masked_best(row_emb, row_label, row_rank, col_emb, col_label, col_rank, want_columns):
    col_count = col_emb.shape[0]
    block_size = math.gcd(512, col_count)
    block_count = col_count // block_size
    emb_blocks = col_emb.reshape(block_count, block_size, col_emb.shape[1])
    label_blocks = col_label.reshape(block_count, block_size)
    rank_blocks = col_rank.reshape(block_count, block_size)

    def visit_block(running, column_piece):
        piece_emb, piece_label, piece_rank = column_piece
        scores = lax.dot_general(
            row_emb, piece_emb, (((1,), (1,)), ((), ())), preferred_element_type=jnp.float32
        )
        same_cluster = (row_label[:, None] == piece_label[None, :]) & (row_label[:, None] >= 0)
        earlier = piece_rank[None, :] < row_rank[:, None]
        row_best = jnp.max(jnp.where(same_cluster & earlier, scores, jnp.float32(-1.0)), axis=1)
        if want_columns:
            later = same_cluster & jnp.logical_not(earlier)
            col_best = jnp.max(jnp.where(later, scores, jnp.float32(-1.0)), axis=0)
        else:
            col_best = jnp.zeros((0,), jnp.float32)
        return (jnp.maximum(running, row_best), col_best)

    initial = jnp.full((row_emb.shape[0],), -1.0, jnp.float32)
    row_best, col_blocks = lax.scan(visit_block, initial, (emb_blocks, label_blocks, rank_blocks))
    return (row_best, col_blocks.reshape(-1))


def body(embeddings, labels, member_rank):
    row_count = embeddings.shape[0]
    feature_count = embeddings.shape[1]
    clus_count = lax.axis_size("clus")
    mem_count = lax.axis_size("mem")
    group_count = clus_count * mem_count
    capacity = 2 * row_count // group_count
    slot_count = group_count * capacity
    group_of = labels // CLUS_GROUP
    one_hot = (group_of[:, None] == jnp.arange(group_count, dtype=jnp.int32)[None, :]).astype(
        jnp.int32
    )
    running_count = jnp.cumsum(one_hot, axis=0) - 1
    within_group = jnp.sum(one_hot * running_count, axis=1)
    slot_of = group_of * capacity + within_group
    send_emb = jnp.zeros((slot_count, feature_count), jnp.bfloat16).at[slot_of].set(embeddings)
    send_label = jnp.full((slot_count,), -1, jnp.int32).at[slot_of].set(labels)
    send_rank = jnp.zeros((slot_count,), jnp.int32).at[slot_of].set(member_rank)
    received = (
        lax.all_to_all(
            send_emb.reshape(group_count, capacity, feature_count),
            ("clus", "mem"),
            split_axis=0,
            concat_axis=0,
            tiled=True,
        ),
        lax.all_to_all(
            send_label.reshape(group_count, capacity),
            ("clus", "mem"),
            split_axis=0,
            concat_axis=0,
            tiled=True,
        ),
        lax.all_to_all(
            send_rank.reshape(group_count, capacity),
            ("clus", "mem"),
            split_axis=0,
            concat_axis=0,
            tiled=True,
        ),
    )
    own_emb = received[0].reshape(slot_count, feature_count)
    own_label = received[1].reshape(slot_count)
    own_rank = received[2].reshape(slot_count)
    other_emb, other_label, other_rank = swapped((own_emb, own_label, own_rank), "sub", 0)
    diag_best, ignored = masked_best(
        own_emb, own_label, own_rank, own_emb, own_label, own_rank, False
    )
    core_side = lax.axis_index("sub")
    is_zero = core_side == 0
    zero_emb = jnp.where(is_zero, own_emb, other_emb)
    zero_label = jnp.where(is_zero, own_label, other_label)
    zero_rank = jnp.where(is_zero, own_rank, other_rank)
    one_emb = jnp.where(is_zero, other_emb, own_emb)
    one_label = jnp.where(is_zero, other_label, own_label)
    one_rank = jnp.where(is_zero, other_rank, own_rank)
    half_count = slot_count // 2
    offset = core_side * half_count
    part_emb = lax.dynamic_slice_in_dim(zero_emb, offset, half_count, 0)
    part_label = lax.dynamic_slice_in_dim(zero_label, offset, half_count, 0)
    part_rank = lax.dynamic_slice_in_dim(zero_rank, offset, half_count, 0)
    half_best, col_part = masked_best(
        part_emb, part_label, part_rank, one_emb, one_label, one_rank, True
    )
    got_half, got_cols = swapped((half_best, col_part), "sub", 0)
    row_side = jnp.concatenate([half_best, got_half])
    cross_best = jnp.where(is_zero, row_side, jnp.maximum(col_part, got_cols))
    nearest = jnp.maximum(diag_best, cross_best)
    returned = lax.all_to_all(
        nearest.reshape(group_count, capacity),
        ("clus", "mem"),
        split_axis=0,
        concat_axis=0,
        tiled=True,
    )
    return returned.reshape(-1)[slot_of]


def local(embeddings, labels, member_rank):
    rows = embeddings.shape[0]
    clus_count, mem_count, sub_count = (lax.axis_size(a) for a in ("clus", "mem", "sub"))
    if fits_kernel(clus_count, mem_count, sub_count, rows):
        return kernel_body(clus_count, mem_count, embeddings, labels, member_rank)
    return body(embeddings, labels, member_rank)


def solution(mesh):
    placed = (
        P(("parts", "clus", "mem", "sub"), None),
        P(("parts", "clus", "mem", "sub")),
        P(("parts", "clus", "mem", "sub")),
    )
    return jax.shard_map(
        local,
        mesh=mesh,
        in_specs=placed,
        out_specs=P(("parts", "clus", "mem", "sub")),
        check_vma=False,
    )
```

```python
import functools
import math

import jax
import jax.numpy as jnp
from jax import lax
from jax.experimental import pallas as pl
from jax.experimental.pallas import tpu as pltpu
from jax.sharding import PartitionSpec as P

CLUS_GROUP = 2
MESH = pl.DeviceIdType.MESH
ROW_TILE = 16
LANES = 128
BYTE = 256
CLASS_STEP = BYTE * BYTE
NO_CAP = 3e38


def flipped(index, mask, size):
    out = 0
    bit = 1
    while bit < size:
        digit = lax.rem(lax.div(index, bit), 2)
        out = out + ((1 - digit) if mask & bit else digit) * bit
        bit *= 2
    return out


def nt_dot(lhs, rhs):
    return lax.dot_general(lhs, rhs, (((1,), (1,)), ((), ())), preferred_element_type=jnp.float32)


def dedup_kernel(
    clus_count,
    mem_count,
    capacity,
    emb_hbm,
    label_hbm,
    rank_hbm,
    out_ref,
    emb,
    label_ref,
    rank_ref,
    caps_own,
    caps_sib,
    send,
    own,
    sib,
    key_out,
    key_in,
    key_own,
    key_sib,
    ret_out,
    ret_in,
    load_sem,
    emb_send,
    emb_recv,
    key_send,
    key_recv,
    fwd_send,
    fwd_recv,
    kf_send,
    kf_recv,
    ret_send,
    ret_recv,
):
    groups = clus_count * mem_count
    rows = emb.shape[0]
    slots = groups * capacity
    tiles = slots // LANES
    per_tile = LANES // capacity
    clus = lax.axis_index("clus")
    mem = lax.axis_index("mem")
    sub = lax.axis_index("sub")
    me = clus * mem_count + mem


    def partner(k):
        return {
            "clus": flipped(clus, k // mem_count, clus_count),
            "mem": flipped(mem, k % mem_count, mem_count),
        }

    sibling = {"sub": 1 - sub}
    load_label = pltpu.make_async_copy(label_hbm, label_ref, load_sem.at[0])
    load_rank = pltpu.make_async_copy(rank_hbm, rank_ref, load_sem.at[1])
    load = pltpu.make_async_copy(emb_hbm, emb, load_sem.at[2])
    load_label.start()
    load.start()
    load_rank.start()
    far_first = list(range(groups - 1, 0, -1))
    barrier = pltpu.get_barrier_semaphore()
    for k in far_first:
        pl.semaphore_signal(barrier, inc=1, device_id=partner(k), device_id_type=MESH)
    pl.semaphore_signal(barrier, inc=1, device_id=sibling, device_id_type=MESH)

    load_label.wait()
    labels = label_ref[...]
    group = lax.div(labels, CLUS_GROUP)
    relative = jnp.bitwise_xor(group, me)
    group_iota = lax.broadcasted_iota(jnp.int32, (groups, rows), 0)
    member = group_iota == relative
    before = lax.broadcasted_iota(jnp.int32, (rows, rows), 0) < lax.broadcasted_iota(
        jnp.int32, (rows, rows), 1
    )
    counts = jnp.dot(
        member.astype(jnp.float32).astype(jnp.bfloat16),
        before.astype(jnp.float32).astype(jnp.bfloat16),
        preferred_element_type=jnp.float32,
    )
    slot = jnp.sum(
        jnp.where(member, counts + (group_iota * capacity).astype(jnp.float32), 0.0),
        axis=0,
        keepdims=True,
    ).astype(jnp.int32)
    place = (
        (lax.broadcasted_iota(jnp.int32, (slots, rows), 0) == slot)
        .astype(jnp.float32)
        .astype(jnp.bfloat16)
    )

    load.wait()

    def fill(first, count):
        span = pl.ds(first * capacity, count * capacity)
        send[span, :] = jnp.dot(
            place[first * capacity : (first + count) * capacity],
            emb[...],
            preferred_element_type=jnp.float32,
        ).astype(jnp.bfloat16)

    def block(ref, k):
        return ref.at[pl.ds(k * capacity, capacity), :]

    emb_copies, key_copies = {}, {}
    for k in far_first:
        emb_copies[k] = pltpu.make_async_remote_copy(
            src_ref=block(send, k),
            dst_ref=block(own, k),
            send_sem=emb_send.at[k],
            recv_sem=emb_recv.at[k],
            device_id=partner(k),
            device_id_type=MESH,
        )
        key_copies[k] = pltpu.make_async_remote_copy(
            src_ref=key_out.at[k // per_tile],
            dst_ref=key_in.at[k],
            send_sem=key_send.at[k],
            recv_sem=key_recv.at[k],
            device_id=partner(k),
            device_id_type=MESH,
        )
    half = groups // 2
    fill(half, half)
    pl.semaphore_wait(barrier, groups)
    for k in far_first[:half]:
        emb_copies[k].start()
    load_rank.wait()
    ranks = rank_ref[...]
    row_iota = lax.broadcasted_iota(jnp.int32, (8, rows), 0)
    digits = jnp.where(
        row_iota == 0,
        labels - group * CLUS_GROUP + 1,
        jnp.where(
            row_iota == 1,
            lax.div(ranks, BYTE),
            jnp.where(row_iota == 2, lax.rem(ranks, BYTE), 0),
        ),
    )
    placed = nt_dot(digits.astype(jnp.float32).astype(jnp.bfloat16), place)
    keys = placed[0:1] * float(CLASS_STEP) + placed[1:2] * float(BYTE) + placed[2:3]
    for t in range(tiles):
        key_out[t] = keys[:, t * LANES : (t + 1) * LANES]
    for k in far_first:
        key_copies[k].start()
    fill(0, half)
    for k in far_first[half:]:
        emb_copies[k].start()
    own[pl.ds(0, capacity), :] = send[pl.ds(0, capacity), :]

    forwards = {}
    for k in range(groups):
        forwards[k] = pltpu.make_async_remote_copy(
            src_ref=block(send if k == 0 else own, k),
            dst_ref=block(sib, k),
            send_sem=fwd_send.at[k],
            recv_sem=fwd_recv.at[k],
            device_id=sibling,
            device_id_type=MESH,
        )
    forwards[0].start()
    lane_block = lax.div(lax.broadcasted_iota(jnp.int32, (1, LANES), 1), capacity)
    for k in range(1, groups):
        key_copies[k].wait_recv()
    for t in range(tiles):
        row = jnp.zeros((1, LANES), jnp.float32)
        for k in range(t * per_tile, (t + 1) * per_tile):
            piece = key_out[t] if k == 0 else key_in[k]
            row = jnp.where(lane_block == k % per_tile, piece, row)
        key_own[t] = row
    key_forward = pltpu.make_async_remote_copy(
        src_ref=key_own,
        dst_ref=key_sib,
        send_sem=kf_send,
        recv_sem=kf_recv,
        device_id=sibling,
        device_id_type=MESH,
    )
    key_forward.start()
    row_keys = jnp.concatenate([key_own[t] for t in range(tiles)], axis=1)
    row_base = (
        lax.div(row_keys.astype(jnp.int32), CLASS_STEP) * CLASS_STEP
    ).astype(jnp.float32)
    row_base = jnp.maximum(row_base, 1.0)

    def make_caps(caps, cand_keys):
        for t in range(tiles):
            column = jnp.transpose(jnp.broadcast_to(cand_keys[t], (LANES, LANES)))
            column = jnp.concatenate([column] * tiles, axis=1)
            allowed = (column < row_keys) & (column >= row_base)
            caps[pl.ds(t * LANES, LANES), :] = jnp.where(allowed, NO_CAP, -1.0)

    make_caps(caps_own, key_own)
    key_forward.wait_recv()
    make_caps(caps_sib, key_sib)

    def masked(cands, caps, first, count):
        span = pl.ds(first * capacity, count * capacity)
        scores = jnp.minimum(nt_dot(cands[span, :], own[...]), caps[span, :])
        return jnp.max(scores, axis=0, keepdims=True)

    for k in range(1, groups):
        emb_copies[k].wait_recv()
        forwards[k].start()
    best = jnp.maximum(masked(own, caps_own, 0, groups), -1.0)
    for first in (0, half):
        for k in range(first, first + half):
            forwards[k].wait_recv()
        best = jnp.maximum(best, masked(sib, caps_sib, first, half))
    for t in range(tiles):
        ret_out[t] = best[:, t * LANES : (t + 1) * LANES]

    returns = {}
    for k in far_first:
        returns[k] = pltpu.make_async_remote_copy(
            src_ref=ret_out.at[k // per_tile],
            dst_ref=ret_in.at[k],
            send_sem=ret_send.at[k],
            recv_sem=ret_recv.at[k],
            device_id=partner(k),
            device_id_type=MESH,
        )
        returns[k].start()
    for k in far_first:
        emb_copies[k].wait_send()
        key_copies[k].wait_send()
    for k in range(groups):
        forwards[k].wait_send()
    key_forward.wait_send()
    for k in range(1, groups):
        returns[k].wait_recv()

    pieces = []
    for t in range(tiles):
        row = jnp.zeros((1, LANES), jnp.float32)
        for k in range(t * per_tile, (t + 1) * per_tile):
            piece = ret_out[t] if k == 0 else ret_in[k]
            row = jnp.where(lane_block == k % per_tile, piece, row)
        pieces.append(row)
    result = jnp.concatenate(pieces, axis=1)
    high = result.astype(jnp.bfloat16).astype(jnp.float32)
    middle = (result - high).astype(jnp.bfloat16).astype(jnp.float32)
    low = result - high - middle
    split_iota = lax.broadcasted_iota(jnp.int32, (8, slots), 0)
    split = jnp.where(
        split_iota == 0,
        high,
        jnp.where(split_iota == 1, middle, jnp.where(split_iota == 2, low, 0.0)),
    ).astype(jnp.bfloat16)
    taken = jnp.dot(split, place, preferred_element_type=jnp.float32)
    out_ref[...] = taken
    for k in far_first:
        returns[k].wait_send()


def kernel_body(clus_count, mem_count, embeddings, labels, member_rank):
    rows, width = embeddings.shape
    groups = clus_count * mem_count
    capacity = 2 * rows // groups
    slots = groups * capacity
    tiles = slots // LANES
    dma = pltpu.SemaphoreType.DMA
    vmem = pl.BlockSpec(memory_space=pltpu.VMEM)
    out = pl.pallas_call(
        functools.partial(dedup_kernel, clus_count, mem_count, capacity),
        out_shape=jax.ShapeDtypeStruct((8, rows), jnp.float32),
        in_specs=[pl.BlockSpec(memory_space=pl.ANY)] * 3,
        out_specs=vmem,
        scratch_shapes=[
            pltpu.VMEM((rows, width), jnp.bfloat16),
            pltpu.VMEM((1, rows), jnp.int32),
            pltpu.VMEM((1, rows), jnp.int32),
            pltpu.VMEM((slots, slots), jnp.float32),
            pltpu.VMEM((slots, slots), jnp.float32),
            pltpu.VMEM((slots, width), jnp.bfloat16),
            pltpu.VMEM((slots, width), jnp.bfloat16),
            pltpu.VMEM((slots, width), jnp.bfloat16),
            pltpu.VMEM((tiles, 1, LANES), jnp.float32),
            pltpu.VMEM((groups, 1, LANES), jnp.float32),
            pltpu.VMEM((tiles, 1, LANES), jnp.float32),
            pltpu.VMEM((tiles, 1, LANES), jnp.float32),
            pltpu.VMEM((tiles, 1, LANES), jnp.float32),
            pltpu.VMEM((groups, 1, LANES), jnp.float32),
            dma((3,)),
            dma((groups,)),
            dma((groups,)),
            dma((groups,)),
            dma((groups,)),
            dma((groups,)),
            dma((groups,)),
            dma,
            dma,
            dma((groups,)),
            dma((groups,)),
        ],
        compiler_params=pltpu.CompilerParams(collective_id=0, has_side_effects=True),
    )(embeddings, labels.reshape(1, rows), member_rank.reshape(1, rows))
    return out[0] + out[1] + out[2]


def fits_kernel(clus_count, mem_count, sub_count, rows):
    groups = clus_count * mem_count
    capacity = 2 * rows // groups
    return (
        clus_count & (clus_count - 1) == 0
        and mem_count & (mem_count - 1) == 0
        and sub_count == 2
        and groups >= 2
        and rows % LANES == 0
        and capacity % ROW_TILE == 0
        and LANES % capacity == 0
        and rows * groups * sub_count <= CLASS_STEP
    )


def swapped(value, axis, stride):
    mask = 2**stride
    pairs = [(source, source ^ mask) for source in range(lax.axis_size(axis))]
    return lax.ppermute(value, axis, pairs)


def masked_best(row_emb, row_label, row_rank, col_emb, col_label, col_rank, want_columns):
    col_count = col_emb.shape[0]
    block_size = math.gcd(512, col_count)
    block_count = col_count // block_size
    emb_blocks = col_emb.reshape(block_count, block_size, col_emb.shape[1])
    label_blocks = col_label.reshape(block_count, block_size)
    rank_blocks = col_rank.reshape(block_count, block_size)

    def visit_block(running, column_piece):
        piece_emb, piece_label, piece_rank = column_piece
        scores = lax.dot_general(
            row_emb, piece_emb, (((1,), (1,)), ((), ())), preferred_element_type=jnp.float32
        )
        same_cluster = (row_label[:, None] == piece_label[None, :]) & (row_label[:, None] >= 0)
        earlier = piece_rank[None, :] < row_rank[:, None]
        row_best = jnp.max(jnp.where(same_cluster & earlier, scores, jnp.float32(-1.0)), axis=1)
        if want_columns:
            later = same_cluster & jnp.logical_not(earlier)
            col_best = jnp.max(jnp.where(later, scores, jnp.float32(-1.0)), axis=0)
        else:
            col_best = jnp.zeros((0,), jnp.float32)
        return (jnp.maximum(running, row_best), col_best)

    initial = jnp.full((row_emb.shape[0],), -1.0, jnp.float32)
    row_best, col_blocks = lax.scan(visit_block, initial, (emb_blocks, label_blocks, rank_blocks))
    return (row_best, col_blocks.reshape(-1))


def body(embeddings, labels, member_rank):
    row_count = embeddings.shape[0]
    feature_count = embeddings.shape[1]
    clus_count = lax.axis_size("clus")
    mem_count = lax.axis_size("mem")
    group_count = clus_count * mem_count
    capacity = 2 * row_count // group_count
    slot_count = group_count * capacity
    group_of = labels // CLUS_GROUP
    one_hot = (group_of[:, None] == jnp.arange(group_count, dtype=jnp.int32)[None, :]).astype(
        jnp.int32
    )
    running_count = jnp.cumsum(one_hot, axis=0) - 1
    within_group = jnp.sum(one_hot * running_count, axis=1)
    slot_of = group_of * capacity + within_group
    send_emb = jnp.zeros((slot_count, feature_count), jnp.bfloat16).at[slot_of].set(embeddings)
    send_label = jnp.full((slot_count,), -1, jnp.int32).at[slot_of].set(labels)
    send_rank = jnp.zeros((slot_count,), jnp.int32).at[slot_of].set(member_rank)
    received = (
        lax.all_to_all(
            send_emb.reshape(group_count, capacity, feature_count),
            ("clus", "mem"),
            split_axis=0,
            concat_axis=0,
            tiled=True,
        ),
        lax.all_to_all(
            send_label.reshape(group_count, capacity),
            ("clus", "mem"),
            split_axis=0,
            concat_axis=0,
            tiled=True,
        ),
        lax.all_to_all(
            send_rank.reshape(group_count, capacity),
            ("clus", "mem"),
            split_axis=0,
            concat_axis=0,
            tiled=True,
        ),
    )
    own_emb = received[0].reshape(slot_count, feature_count)
    own_label = received[1].reshape(slot_count)
    own_rank = received[2].reshape(slot_count)
    other_emb, other_label, other_rank = swapped((own_emb, own_label, own_rank), "sub", 0)
    diag_best, ignored = masked_best(
        own_emb, own_label, own_rank, own_emb, own_label, own_rank, False
    )
    core_side = lax.axis_index("sub")
    is_zero = core_side == 0
    zero_emb = jnp.where(is_zero, own_emb, other_emb)
    zero_label = jnp.where(is_zero, own_label, other_label)
    zero_rank = jnp.where(is_zero, own_rank, other_rank)
    one_emb = jnp.where(is_zero, other_emb, own_emb)
    one_label = jnp.where(is_zero, other_label, own_label)
    one_rank = jnp.where(is_zero, other_rank, own_rank)
    half_count = slot_count // 2
    offset = core_side * half_count
    part_emb = lax.dynamic_slice_in_dim(zero_emb, offset, half_count, 0)
    part_label = lax.dynamic_slice_in_dim(zero_label, offset, half_count, 0)
    part_rank = lax.dynamic_slice_in_dim(zero_rank, offset, half_count, 0)
    half_best, col_part = masked_best(
        part_emb, part_label, part_rank, one_emb, one_label, one_rank, True
    )
    got_half, got_cols = swapped((half_best, col_part), "sub", 0)
    row_side = jnp.concatenate([half_best, got_half])
    cross_best = jnp.where(is_zero, row_side, jnp.maximum(col_part, got_cols))
    nearest = jnp.maximum(diag_best, cross_best)
    returned = lax.all_to_all(
        nearest.reshape(group_count, capacity),
        ("clus", "mem"),
        split_axis=0,
        concat_axis=0,
        tiled=True,
    )
    return returned.reshape(-1)[slot_of]


def local(embeddings, labels, member_rank):
    rows = embeddings.shape[0]
    clus_count, mem_count, sub_count = (lax.axis_size(a) for a in ("clus", "mem", "sub"))
    if fits_kernel(clus_count, mem_count, sub_count, rows):
        return kernel_body(clus_count, mem_count, embeddings, labels, member_rank)
    return body(embeddings, labels, member_rank)


def solution(mesh):
    placed = (
        P(("parts", "clus", "mem", "sub"), None),
        P(("parts", "clus", "mem", "sub")),
        P(("parts", "clus", "mem", "sub")),
    )
    return jax.shard_map(
        local,
        mesh=mesh,
        in_specs=placed,
        out_specs=P(("parts", "clus", "mem", "sub")),
        check_vma=False,
    )
```

```python
import functools
import math

import jax
import jax.numpy as jnp
from jax import lax
from jax.experimental import pallas as pl
from jax.experimental.pallas import tpu as pltpu
from jax.sharding import PartitionSpec as P

CLUS_GROUP = 2
MESH = pl.DeviceIdType.MESH
ROW_TILE = 16
LANES = 128
BYTE = 256
CLASS_STEP = BYTE * BYTE
NO_CAP = 3e38


def flipped(index, mask, size):
    out = 0
    bit = 1
    while bit < size:
        digit = lax.rem(lax.div(index, bit), 2)
        out = out + ((1 - digit) if mask & bit else digit) * bit
        bit *= 2
    return out


def nt_dot(lhs, rhs):
    return lax.dot_general(lhs, rhs, (((1,), (1,)), ((), ())), preferred_element_type=jnp.float32)


def dedup_kernel(
    clus_count,
    mem_count,
    capacity,
    emb_hbm,
    label_hbm,
    rank_hbm,
    out_ref,
    emb,
    label_ref,
    rank_ref,
    caps_own,
    caps_sib,
    send,
    own,
    sib,
    key_out,
    key_in,
    key_own,
    key_sib,
    ret_out,
    ret_in,
    load_sem,
    emb_send,
    emb_recv,
    key_send,
    key_recv,
    fwd_send,
    fwd_recv,
    kf_send,
    kf_recv,
    ret_send,
    ret_recv,
):
    groups = clus_count * mem_count
    rows = emb.shape[0]
    slots = groups * capacity
    tiles = slots // LANES
    per_tile = LANES // capacity
    clus = lax.axis_index("clus")
    mem = lax.axis_index("mem")
    sub = lax.axis_index("sub")
    me = clus * mem_count + mem


    def partner(k):
        return {
            "clus": flipped(clus, k // mem_count, clus_count),
            "mem": flipped(mem, k % mem_count, mem_count),
        }

    sibling = {"sub": 1 - sub}
    load_label = pltpu.make_async_copy(label_hbm, label_ref, load_sem.at[0])
    load_rank = pltpu.make_async_copy(rank_hbm, rank_ref, load_sem.at[1])
    load = pltpu.make_async_copy(emb_hbm, emb, load_sem.at[2])
    load_label.start()
    load.start()
    load_rank.start()
    far_first = list(range(groups - 1, 0, -1))
    barrier = pltpu.get_barrier_semaphore()
    for k in far_first:
        pl.semaphore_signal(barrier, inc=1, device_id=partner(k), device_id_type=MESH)
    pl.semaphore_signal(barrier, inc=1, device_id=sibling, device_id_type=MESH)

    load_label.wait()
    labels = label_ref[...]
    group = lax.div(labels, CLUS_GROUP)
    relative = jnp.bitwise_xor(group, me)
    group_iota = lax.broadcasted_iota(jnp.int32, (groups, rows), 0)
    member = group_iota == relative
    before = lax.broadcasted_iota(jnp.int32, (rows, rows), 0) < lax.broadcasted_iota(
        jnp.int32, (rows, rows), 1
    )
    counts = jnp.dot(
        member.astype(jnp.float32).astype(jnp.bfloat16),
        before.astype(jnp.float32).astype(jnp.bfloat16),
        preferred_element_type=jnp.float32,
    )
    slot = jnp.sum(
        jnp.where(member, counts + (group_iota * capacity).astype(jnp.float32), 0.0),
        axis=0,
        keepdims=True,
    ).astype(jnp.int32)
    place = (
        (lax.broadcasted_iota(jnp.int32, (slots, rows), 0) == slot)
        .astype(jnp.float32)
        .astype(jnp.bfloat16)
    )

    def fill(first, count):
        span = pl.ds(first * capacity, count * capacity)
        send[span, :] = jnp.dot(
            place[first * capacity : (first + count) * capacity],
            emb[...],
            preferred_element_type=jnp.float32,
        ).astype(jnp.bfloat16)

    def block(ref, k):
        return ref.at[pl.ds(k * capacity, capacity), :]

    emb_copies, key_copies = {}, {}
    for k in far_first:
        emb_copies[k] = pltpu.make_async_remote_copy(
            src_ref=block(send, k),
            dst_ref=block(own, k),
            send_sem=emb_send.at[k],
            recv_sem=emb_recv.at[k],
            device_id=partner(k),
            device_id_type=MESH,
        )
        key_copies[k] = pltpu.make_async_remote_copy(
            src_ref=key_out.at[k // per_tile],
            dst_ref=key_in.at[k],
            send_sem=key_send.at[k],
            recv_sem=key_recv.at[k],
            device_id=partner(k),
            device_id_type=MESH,
        )
    half = groups // 2
    load_rank.wait()
    ranks = rank_ref[...]
    row_iota = lax.broadcasted_iota(jnp.int32, (8, rows), 0)
    digits = jnp.where(
        row_iota == 0,
        labels - group * CLUS_GROUP + 1,
        jnp.where(
            row_iota == 1,
            lax.div(ranks, BYTE),
            jnp.where(row_iota == 2, lax.rem(ranks, BYTE), 0),
        ),
    )
    placed = nt_dot(digits.astype(jnp.float32).astype(jnp.bfloat16), place)
    keys = placed[0:1] * float(CLASS_STEP) + placed[1:2] * float(BYTE) + placed[2:3]
    for t in range(tiles):
        key_out[t] = keys[:, t * LANES : (t + 1) * LANES]
    load.wait()
    fill(half, half)
    pl.semaphore_wait(barrier, groups)
    for k in far_first:
        key_copies[k].start()
    for k in far_first[:half]:
        emb_copies[k].start()
    fill(0, half)
    for k in far_first[half:]:
        emb_copies[k].start()
    own[pl.ds(0, capacity), :] = send[pl.ds(0, capacity), :]

    forwards = {}
    for k in range(groups):
        forwards[k] = pltpu.make_async_remote_copy(
            src_ref=block(send if k == 0 else own, k),
            dst_ref=block(sib, k),
            send_sem=fwd_send.at[k],
            recv_sem=fwd_recv.at[k],
            device_id=sibling,
            device_id_type=MESH,
        )
    forwards[0].start()
    lane_block = lax.div(lax.broadcasted_iota(jnp.int32, (1, LANES), 1), capacity)
    for k in range(1, groups):
        key_copies[k].wait_recv()
    for t in range(tiles):
        row = jnp.zeros((1, LANES), jnp.float32)
        for k in range(t * per_tile, (t + 1) * per_tile):
            piece = key_out[t] if k == 0 else key_in[k]
            row = jnp.where(lane_block == k % per_tile, piece, row)
        key_own[t] = row
    key_forward = pltpu.make_async_remote_copy(
        src_ref=key_own,
        dst_ref=key_sib,
        send_sem=kf_send,
        recv_sem=kf_recv,
        device_id=sibling,
        device_id_type=MESH,
    )
    key_forward.start()
    row_keys = jnp.concatenate([key_own[t] for t in range(tiles)], axis=1)
    row_base = (
        lax.div(row_keys.astype(jnp.int32), CLASS_STEP) * CLASS_STEP
    ).astype(jnp.float32)
    row_base = jnp.maximum(row_base, 1.0)

    def make_caps(caps, cand_keys):
        for t in range(tiles):
            column = jnp.transpose(jnp.broadcast_to(cand_keys[t], (LANES, LANES)))
            column = jnp.concatenate([column] * tiles, axis=1)
            allowed = (column < row_keys) & (column >= row_base)
            caps[pl.ds(t * LANES, LANES), :] = jnp.where(allowed, NO_CAP, -1.0)

    make_caps(caps_own, key_own)
    key_forward.wait_recv()
    make_caps(caps_sib, key_sib)

    def masked(cands, caps, first, count):
        span = pl.ds(first * capacity, count * capacity)
        scores = jnp.minimum(nt_dot(cands[span, :], own[...]), caps[span, :])
        return jnp.max(scores, axis=0, keepdims=True)

    for k in range(1, groups):
        emb_copies[k].wait_recv()
        forwards[k].start()
    best = jnp.maximum(masked(own, caps_own, 0, groups), -1.0)
    for first in (0, half):
        for k in range(first, first + half):
            forwards[k].wait_recv()
        best = jnp.maximum(best, masked(sib, caps_sib, first, half))
    for t in range(tiles):
        ret_out[t] = best[:, t * LANES : (t + 1) * LANES]

    returns = {}
    for k in far_first:
        returns[k] = pltpu.make_async_remote_copy(
            src_ref=ret_out.at[k // per_tile],
            dst_ref=ret_in.at[k],
            send_sem=ret_send.at[k],
            recv_sem=ret_recv.at[k],
            device_id=partner(k),
            device_id_type=MESH,
        )
        returns[k].start()
    for k in far_first:
        emb_copies[k].wait_send()
        key_copies[k].wait_send()
    for k in range(groups):
        forwards[k].wait_send()
    key_forward.wait_send()
    for k in range(1, groups):
        returns[k].wait_recv()

    pieces = []
    for t in range(tiles):
        row = jnp.zeros((1, LANES), jnp.float32)
        for k in range(t * per_tile, (t + 1) * per_tile):
            piece = ret_out[t] if k == 0 else ret_in[k]
            row = jnp.where(lane_block == k % per_tile, piece, row)
        pieces.append(row)
    result = jnp.concatenate(pieces, axis=1)
    high = result.astype(jnp.bfloat16).astype(jnp.float32)
    middle = (result - high).astype(jnp.bfloat16).astype(jnp.float32)
    low = result - high - middle
    split_iota = lax.broadcasted_iota(jnp.int32, (8, slots), 0)
    split = jnp.where(
        split_iota == 0,
        high,
        jnp.where(split_iota == 1, middle, jnp.where(split_iota == 2, low, 0.0)),
    ).astype(jnp.bfloat16)
    taken = jnp.dot(split, place, preferred_element_type=jnp.float32)
    out_ref[...] = taken[0:1] + taken[1:2] + taken[2:3]
    for k in far_first:
        returns[k].wait_send()


def kernel_body(clus_count, mem_count, embeddings, labels, member_rank):
    rows, width = embeddings.shape
    groups = clus_count * mem_count
    capacity = 2 * rows // groups
    slots = groups * capacity
    tiles = slots // LANES
    dma = pltpu.SemaphoreType.DMA
    vmem = pl.BlockSpec(memory_space=pltpu.VMEM)
    out = pl.pallas_call(
        functools.partial(dedup_kernel, clus_count, mem_count, capacity),
        out_shape=jax.ShapeDtypeStruct((1, rows), jnp.float32),
        in_specs=[pl.BlockSpec(memory_space=pl.ANY)] * 3,
        out_specs=vmem,
        scratch_shapes=[
            pltpu.VMEM((rows, width), jnp.bfloat16),
            pltpu.VMEM((1, rows), jnp.int32),
            pltpu.VMEM((1, rows), jnp.int32),
            pltpu.VMEM((slots, slots), jnp.float32),
            pltpu.VMEM((slots, slots), jnp.float32),
            pltpu.VMEM((slots, width), jnp.bfloat16),
            pltpu.VMEM((slots, width), jnp.bfloat16),
            pltpu.VMEM((slots, width), jnp.bfloat16),
            pltpu.VMEM((tiles, 1, LANES), jnp.float32),
            pltpu.VMEM((groups, 1, LANES), jnp.float32),
            pltpu.VMEM((tiles, 1, LANES), jnp.float32),
            pltpu.VMEM((tiles, 1, LANES), jnp.float32),
            pltpu.VMEM((tiles, 1, LANES), jnp.float32),
            pltpu.VMEM((groups, 1, LANES), jnp.float32),
            dma((3,)),
            dma((groups,)),
            dma((groups,)),
            dma((groups,)),
            dma((groups,)),
            dma((groups,)),
            dma((groups,)),
            dma,
            dma,
            dma((groups,)),
            dma((groups,)),
        ],
        compiler_params=pltpu.CompilerParams(collective_id=0, has_side_effects=True),
    )(embeddings, labels.reshape(1, rows), member_rank.reshape(1, rows))
    return out.reshape(rows)


def fits_kernel(clus_count, mem_count, sub_count, rows):
    groups = clus_count * mem_count
    capacity = 2 * rows // groups
    return (
        clus_count & (clus_count - 1) == 0
        and mem_count & (mem_count - 1) == 0
        and sub_count == 2
        and groups >= 2
        and rows % LANES == 0
        and capacity % ROW_TILE == 0
        and LANES % capacity == 0
        and rows * groups * sub_count <= CLASS_STEP
    )


def swapped(value, axis, stride):
    mask = 2**stride
    pairs = [(source, source ^ mask) for source in range(lax.axis_size(axis))]
    return lax.ppermute(value, axis, pairs)


def masked_best(row_emb, row_label, row_rank, col_emb, col_label, col_rank, want_columns):
    col_count = col_emb.shape[0]
    block_size = math.gcd(512, col_count)
    block_count = col_count // block_size
    emb_blocks = col_emb.reshape(block_count, block_size, col_emb.shape[1])
    label_blocks = col_label.reshape(block_count, block_size)
    rank_blocks = col_rank.reshape(block_count, block_size)

    def visit_block(running, column_piece):
        piece_emb, piece_label, piece_rank = column_piece
        scores = lax.dot_general(
            row_emb, piece_emb, (((1,), (1,)), ((), ())), preferred_element_type=jnp.float32
        )
        same_cluster = (row_label[:, None] == piece_label[None, :]) & (row_label[:, None] >= 0)
        earlier = piece_rank[None, :] < row_rank[:, None]
        row_best = jnp.max(jnp.where(same_cluster & earlier, scores, jnp.float32(-1.0)), axis=1)
        if want_columns:
            later = same_cluster & jnp.logical_not(earlier)
            col_best = jnp.max(jnp.where(later, scores, jnp.float32(-1.0)), axis=0)
        else:
            col_best = jnp.zeros((0,), jnp.float32)
        return (jnp.maximum(running, row_best), col_best)

    initial = jnp.full((row_emb.shape[0],), -1.0, jnp.float32)
    row_best, col_blocks = lax.scan(visit_block, initial, (emb_blocks, label_blocks, rank_blocks))
    return (row_best, col_blocks.reshape(-1))


def body(embeddings, labels, member_rank):
    row_count = embeddings.shape[0]
    feature_count = embeddings.shape[1]
    clus_count = lax.axis_size("clus")
    mem_count = lax.axis_size("mem")
    group_count = clus_count * mem_count
    capacity = 2 * row_count // group_count
    slot_count = group_count * capacity
    group_of = labels // CLUS_GROUP
    one_hot = (group_of[:, None] == jnp.arange(group_count, dtype=jnp.int32)[None, :]).astype(
        jnp.int32
    )
    running_count = jnp.cumsum(one_hot, axis=0) - 1
    within_group = jnp.sum(one_hot * running_count, axis=1)
    slot_of = group_of * capacity + within_group
    send_emb = jnp.zeros((slot_count, feature_count), jnp.bfloat16).at[slot_of].set(embeddings)
    send_label = jnp.full((slot_count,), -1, jnp.int32).at[slot_of].set(labels)
    send_rank = jnp.zeros((slot_count,), jnp.int32).at[slot_of].set(member_rank)
    received = (
        lax.all_to_all(
            send_emb.reshape(group_count, capacity, feature_count),
            ("clus", "mem"),
            split_axis=0,
            concat_axis=0,
            tiled=True,
        ),
        lax.all_to_all(
            send_label.reshape(group_count, capacity),
            ("clus", "mem"),
            split_axis=0,
            concat_axis=0,
            tiled=True,
        ),
        lax.all_to_all(
            send_rank.reshape(group_count, capacity),
            ("clus", "mem"),
            split_axis=0,
            concat_axis=0,
            tiled=True,
        ),
    )
    own_emb = received[0].reshape(slot_count, feature_count)
    own_label = received[1].reshape(slot_count)
    own_rank = received[2].reshape(slot_count)
    other_emb, other_label, other_rank = swapped((own_emb, own_label, own_rank), "sub", 0)
    diag_best, ignored = masked_best(
        own_emb, own_label, own_rank, own_emb, own_label, own_rank, False
    )
    core_side = lax.axis_index("sub")
    is_zero = core_side == 0
    zero_emb = jnp.where(is_zero, own_emb, other_emb)
    zero_label = jnp.where(is_zero, own_label, other_label)
    zero_rank = jnp.where(is_zero, own_rank, other_rank)
    one_emb = jnp.where(is_zero, other_emb, own_emb)
    one_label = jnp.where(is_zero, other_label, own_label)
    one_rank = jnp.where(is_zero, other_rank, own_rank)
    half_count = slot_count // 2
    offset = core_side * half_count
    part_emb = lax.dynamic_slice_in_dim(zero_emb, offset, half_count, 0)
    part_label = lax.dynamic_slice_in_dim(zero_label, offset, half_count, 0)
    part_rank = lax.dynamic_slice_in_dim(zero_rank, offset, half_count, 0)
    half_best, col_part = masked_best(
        part_emb, part_label, part_rank, one_emb, one_label, one_rank, True
    )
    got_half, got_cols = swapped((half_best, col_part), "sub", 0)
    row_side = jnp.concatenate([half_best, got_half])
    cross_best = jnp.where(is_zero, row_side, jnp.maximum(col_part, got_cols))
    nearest = jnp.maximum(diag_best, cross_best)
    returned = lax.all_to_all(
        nearest.reshape(group_count, capacity),
        ("clus", "mem"),
        split_axis=0,
        concat_axis=0,
        tiled=True,
    )
    return returned.reshape(-1)[slot_of]


def local(embeddings, labels, member_rank):
    rows = embeddings.shape[0]
    clus_count, mem_count, sub_count = (lax.axis_size(a) for a in ("clus", "mem", "sub"))
    if fits_kernel(clus_count, mem_count, sub_count, rows):
        return kernel_body(clus_count, mem_count, embeddings, labels, member_rank)
    return body(embeddings, labels, member_rank)


def solution(mesh):
    placed = (
        P(("parts", "clus", "mem", "sub"), None),
        P(("parts", "clus", "mem", "sub")),
        P(("parts", "clus", "mem", "sub")),
    )
    return jax.shard_map(
        local,
        mesh=mesh,
        in_specs=placed,
        out_specs=P(("parts", "clus", "mem", "sub")),
        check_vma=False,
    )
```

```python
import functools
import math

import jax
import jax.numpy as jnp
from jax import lax
from jax.experimental import pallas as pl
from jax.experimental.pallas import tpu as pltpu
from jax.sharding import PartitionSpec as P

CLUS_GROUP = 2
MESH = pl.DeviceIdType.MESH
ROW_TILE = 16
LANES = 128
BYTE = 256
CLASS_STEP = BYTE * BYTE
NO_CAP = 3e38


def flipped(index, mask, size):
    out = 0
    bit = 1
    while bit < size:
        digit = lax.rem(lax.div(index, bit), 2)
        out = out + ((1 - digit) if mask & bit else digit) * bit
        bit *= 2
    return out


def nt_dot(lhs, rhs):
    return lax.dot_general(lhs, rhs, (((1,), (1,)), ((), ())), preferred_element_type=jnp.float32)


def dedup_kernel(
    clus_count,
    mem_count,
    capacity,
    emb_hbm,
    label_hbm,
    rank_hbm,
    out_ref,
    emb,
    label_ref,
    rank_ref,
    caps_own,
    caps_sib,
    send,
    own,
    sib,
    key_out,
    key_in,
    key_own,
    key_sib,
    ret_out,
    ret_in,
    load_sem,
    emb_send,
    emb_recv,
    key_send,
    key_recv,
    fwd_send,
    fwd_recv,
    kf_send,
    kf_recv,
    ret_send,
    ret_recv,
):
    groups = clus_count * mem_count
    rows = emb.shape[0]
    slots = groups * capacity
    tiles = slots // LANES
    per_tile = LANES // capacity
    clus = lax.axis_index("clus")
    mem = lax.axis_index("mem")
    sub = lax.axis_index("sub")
    me = clus * mem_count + mem


    def partner(k):
        return {
            "clus": flipped(clus, k // mem_count, clus_count),
            "mem": flipped(mem, k % mem_count, mem_count),
        }

    sibling = {"sub": 1 - sub}
    load_label = pltpu.make_async_copy(label_hbm, label_ref, load_sem.at[0])
    load_rank = pltpu.make_async_copy(rank_hbm, rank_ref, load_sem.at[1])
    load = pltpu.make_async_copy(emb_hbm, emb, load_sem.at[2])
    load_label.start()
    load.start()
    load_rank.start()
    far_first = list(range(groups - 1, 0, -1))
    barrier = pltpu.get_barrier_semaphore()
    for k in far_first:
        pl.semaphore_signal(barrier, inc=1, device_id=partner(k), device_id_type=MESH)
    pl.semaphore_signal(barrier, inc=1, device_id=sibling, device_id_type=MESH)

    load_label.wait()
    labels = label_ref[...]
    group = lax.div(labels, CLUS_GROUP)
    relative = jnp.bitwise_xor(group, me)
    group_iota = lax.broadcasted_iota(jnp.int32, (groups, rows), 0)
    member = group_iota == relative
    before = lax.broadcasted_iota(jnp.int32, (rows, rows), 0) < lax.broadcasted_iota(
        jnp.int32, (rows, rows), 1
    )
    counts = jnp.dot(
        member.astype(jnp.float32).astype(jnp.bfloat16),
        before.astype(jnp.float32).astype(jnp.bfloat16),
        preferred_element_type=jnp.float32,
    )
    slot = jnp.sum(
        jnp.where(member, counts + (group_iota * capacity).astype(jnp.float32), 0.0),
        axis=0,
        keepdims=True,
    ).astype(jnp.int32)
    place = (
        (lax.broadcasted_iota(jnp.int32, (slots, rows), 0) == slot)
        .astype(jnp.float32)
        .astype(jnp.bfloat16)
    )

    def fill(first, count):
        span = pl.ds(first * capacity, count * capacity)
        send[span, :] = jnp.dot(
            place[first * capacity : (first + count) * capacity],
            emb[...],
            preferred_element_type=jnp.float32,
        ).astype(jnp.bfloat16)

    def send_order(k):
        clus_mask, mem_mask = divmod(k, mem_count)
        near = clus_mask < clus_count // 2
        return near, -clus_mask if near else clus_mask, -mem_mask

    def block(ref, k):
        return ref.at[pl.ds(k * capacity, capacity), :]

    emb_copies, key_copies = {}, {}
    for k in far_first:
        emb_copies[k] = pltpu.make_async_remote_copy(
            src_ref=block(send, k),
            dst_ref=block(own, k),
            send_sem=emb_send.at[k],
            recv_sem=emb_recv.at[k],
            device_id=partner(k),
            device_id_type=MESH,
        )
        key_copies[k] = pltpu.make_async_remote_copy(
            src_ref=key_out.at[k // per_tile],
            dst_ref=key_in.at[k],
            send_sem=key_send.at[k],
            recv_sem=key_recv.at[k],
            device_id=partner(k),
            device_id_type=MESH,
        )
    half = groups // 2
    load_rank.wait()
    ranks = rank_ref[...]
    row_iota = lax.broadcasted_iota(jnp.int32, (8, rows), 0)
    digits = jnp.where(
        row_iota == 0,
        labels - group * CLUS_GROUP + 1,
        jnp.where(
            row_iota == 1,
            lax.div(ranks, BYTE),
            jnp.where(row_iota == 2, lax.rem(ranks, BYTE), 0),
        ),
    )
    placed = nt_dot(digits.astype(jnp.float32).astype(jnp.bfloat16), place)
    keys = placed[0:1] * float(CLASS_STEP) + placed[1:2] * float(BYTE) + placed[2:3]
    for t in range(tiles):
        key_out[t] = keys[:, t * LANES : (t + 1) * LANES]
    load.wait()
    fill(0, groups)
    pl.semaphore_wait(barrier, groups)
    for k in far_first:
        key_copies[k].start()
    for k in sorted(far_first, key=send_order):
        emb_copies[k].start()
    own[pl.ds(0, capacity), :] = send[pl.ds(0, capacity), :]

    forwards = {}
    for k in range(groups):
        forwards[k] = pltpu.make_async_remote_copy(
            src_ref=block(send if k == 0 else own, k),
            dst_ref=block(sib, k),
            send_sem=fwd_send.at[k],
            recv_sem=fwd_recv.at[k],
            device_id=sibling,
            device_id_type=MESH,
        )
    forwards[0].start()
    lane_block = lax.div(lax.broadcasted_iota(jnp.int32, (1, LANES), 1), capacity)
    for k in range(1, groups):
        key_copies[k].wait_recv()
    for t in range(tiles):
        row = jnp.zeros((1, LANES), jnp.float32)
        for k in range(t * per_tile, (t + 1) * per_tile):
            piece = key_out[t] if k == 0 else key_in[k]
            row = jnp.where(lane_block == k % per_tile, piece, row)
        key_own[t] = row
    key_forward = pltpu.make_async_remote_copy(
        src_ref=key_own,
        dst_ref=key_sib,
        send_sem=kf_send,
        recv_sem=kf_recv,
        device_id=sibling,
        device_id_type=MESH,
    )
    key_forward.start()
    row_keys = jnp.concatenate([key_own[t] for t in range(tiles)], axis=1)
    row_base = (
        lax.div(row_keys.astype(jnp.int32), CLASS_STEP) * CLASS_STEP
    ).astype(jnp.float32)
    row_base = jnp.maximum(row_base, 1.0)

    def make_caps(caps, cand_keys):
        for t in range(tiles):
            column = jnp.transpose(jnp.broadcast_to(cand_keys[t], (LANES, LANES)))
            column = jnp.concatenate([column] * tiles, axis=1)
            allowed = (column < row_keys) & (column >= row_base)
            caps[pl.ds(t * LANES, LANES), :] = jnp.where(allowed, NO_CAP, -1.0)

    make_caps(caps_own, key_own)
    key_forward.wait_recv()
    make_caps(caps_sib, key_sib)

    def masked(cands, caps, first, count):
        span = pl.ds(first * capacity, count * capacity)
        scores = jnp.minimum(nt_dot(cands[span, :], own[...]), caps[span, :])
        return jnp.max(scores, axis=0, keepdims=True)

    for k in range(1, groups):
        emb_copies[k].wait_recv()
        forwards[k].start()
    best = jnp.maximum(masked(own, caps_own, 0, groups), -1.0)
    for first in (0, half):
        for k in range(first, first + half):
            forwards[k].wait_recv()
        best = jnp.maximum(best, masked(sib, caps_sib, first, half))
    for t in range(tiles):
        ret_out[t] = best[:, t * LANES : (t + 1) * LANES]

    returns = {}
    for k in far_first:
        returns[k] = pltpu.make_async_remote_copy(
            src_ref=ret_out.at[k // per_tile],
            dst_ref=ret_in.at[k],
            send_sem=ret_send.at[k],
            recv_sem=ret_recv.at[k],
            device_id=partner(k),
            device_id_type=MESH,
        )
        returns[k].start()
    for k in far_first:
        emb_copies[k].wait_send()
        key_copies[k].wait_send()
    for k in range(groups):
        forwards[k].wait_send()
    key_forward.wait_send()
    for k in range(1, groups):
        returns[k].wait_recv()

    pieces = []
    for t in range(tiles):
        row = jnp.zeros((1, LANES), jnp.float32)
        for k in range(t * per_tile, (t + 1) * per_tile):
            piece = ret_out[t] if k == 0 else ret_in[k]
            row = jnp.where(lane_block == k % per_tile, piece, row)
        pieces.append(row)
    result = jnp.concatenate(pieces, axis=1)
    high = result.astype(jnp.bfloat16).astype(jnp.float32)
    middle = (result - high).astype(jnp.bfloat16).astype(jnp.float32)
    low = result - high - middle
    split_iota = lax.broadcasted_iota(jnp.int32, (8, slots), 0)
    split = jnp.where(
        split_iota == 0,
        high,
        jnp.where(split_iota == 1, middle, jnp.where(split_iota == 2, low, 0.0)),
    ).astype(jnp.bfloat16)
    taken = jnp.dot(split, place, preferred_element_type=jnp.float32)
    out_ref[...] = taken[0:1] + taken[1:2] + taken[2:3]
    for k in far_first:
        returns[k].wait_send()


def kernel_body(clus_count, mem_count, embeddings, labels, member_rank):
    rows, width = embeddings.shape
    groups = clus_count * mem_count
    capacity = 2 * rows // groups
    slots = groups * capacity
    tiles = slots // LANES
    dma = pltpu.SemaphoreType.DMA
    vmem = pl.BlockSpec(memory_space=pltpu.VMEM)
    out = pl.pallas_call(
        functools.partial(dedup_kernel, clus_count, mem_count, capacity),
        out_shape=jax.ShapeDtypeStruct((1, rows), jnp.float32),
        in_specs=[pl.BlockSpec(memory_space=pl.ANY)] * 3,
        out_specs=vmem,
        scratch_shapes=[
            pltpu.VMEM((rows, width), jnp.bfloat16),
            pltpu.VMEM((1, rows), jnp.int32),
            pltpu.VMEM((1, rows), jnp.int32),
            pltpu.VMEM((slots, slots), jnp.float32),
            pltpu.VMEM((slots, slots), jnp.float32),
            pltpu.VMEM((slots, width), jnp.bfloat16),
            pltpu.VMEM((slots, width), jnp.bfloat16),
            pltpu.VMEM((slots, width), jnp.bfloat16),
            pltpu.VMEM((tiles, 1, LANES), jnp.float32),
            pltpu.VMEM((groups, 1, LANES), jnp.float32),
            pltpu.VMEM((tiles, 1, LANES), jnp.float32),
            pltpu.VMEM((tiles, 1, LANES), jnp.float32),
            pltpu.VMEM((tiles, 1, LANES), jnp.float32),
            pltpu.VMEM((groups, 1, LANES), jnp.float32),
            dma((3,)),
            dma((groups,)),
            dma((groups,)),
            dma((groups,)),
            dma((groups,)),
            dma((groups,)),
            dma((groups,)),
            dma,
            dma,
            dma((groups,)),
            dma((groups,)),
        ],
        compiler_params=pltpu.CompilerParams(collective_id=0, has_side_effects=True),
    )(embeddings, labels.reshape(1, rows), member_rank.reshape(1, rows))
    return out.reshape(rows)


def fits_kernel(clus_count, mem_count, sub_count, rows):
    groups = clus_count * mem_count
    capacity = 2 * rows // groups
    return (
        clus_count & (clus_count - 1) == 0
        and mem_count & (mem_count - 1) == 0
        and sub_count == 2
        and groups >= 2
        and rows % LANES == 0
        and capacity % ROW_TILE == 0
        and LANES % capacity == 0
        and rows * groups * sub_count <= CLASS_STEP
    )


def swapped(value, axis, stride):
    mask = 2**stride
    pairs = [(source, source ^ mask) for source in range(lax.axis_size(axis))]
    return lax.ppermute(value, axis, pairs)


def masked_best(row_emb, row_label, row_rank, col_emb, col_label, col_rank, want_columns):
    col_count = col_emb.shape[0]
    block_size = math.gcd(512, col_count)
    block_count = col_count // block_size
    emb_blocks = col_emb.reshape(block_count, block_size, col_emb.shape[1])
    label_blocks = col_label.reshape(block_count, block_size)
    rank_blocks = col_rank.reshape(block_count, block_size)

    def visit_block(running, column_piece):
        piece_emb, piece_label, piece_rank = column_piece
        scores = lax.dot_general(
            row_emb, piece_emb, (((1,), (1,)), ((), ())), preferred_element_type=jnp.float32
        )
        same_cluster = (row_label[:, None] == piece_label[None, :]) & (row_label[:, None] >= 0)
        earlier = piece_rank[None, :] < row_rank[:, None]
        row_best = jnp.max(jnp.where(same_cluster & earlier, scores, jnp.float32(-1.0)), axis=1)
        if want_columns:
            later = same_cluster & jnp.logical_not(earlier)
            col_best = jnp.max(jnp.where(later, scores, jnp.float32(-1.0)), axis=0)
        else:
            col_best = jnp.zeros((0,), jnp.float32)
        return (jnp.maximum(running, row_best), col_best)

    initial = jnp.full((row_emb.shape[0],), -1.0, jnp.float32)
    row_best, col_blocks = lax.scan(visit_block, initial, (emb_blocks, label_blocks, rank_blocks))
    return (row_best, col_blocks.reshape(-1))


def body(embeddings, labels, member_rank):
    row_count = embeddings.shape[0]
    feature_count = embeddings.shape[1]
    clus_count = lax.axis_size("clus")
    mem_count = lax.axis_size("mem")
    group_count = clus_count * mem_count
    capacity = 2 * row_count // group_count
    slot_count = group_count * capacity
    group_of = labels // CLUS_GROUP
    one_hot = (group_of[:, None] == jnp.arange(group_count, dtype=jnp.int32)[None, :]).astype(
        jnp.int32
    )
    running_count = jnp.cumsum(one_hot, axis=0) - 1
    within_group = jnp.sum(one_hot * running_count, axis=1)
    slot_of = group_of * capacity + within_group
    send_emb = jnp.zeros((slot_count, feature_count), jnp.bfloat16).at[slot_of].set(embeddings)
    send_label = jnp.full((slot_count,), -1, jnp.int32).at[slot_of].set(labels)
    send_rank = jnp.zeros((slot_count,), jnp.int32).at[slot_of].set(member_rank)
    received = (
        lax.all_to_all(
            send_emb.reshape(group_count, capacity, feature_count),
            ("clus", "mem"),
            split_axis=0,
            concat_axis=0,
            tiled=True,
        ),
        lax.all_to_all(
            send_label.reshape(group_count, capacity),
            ("clus", "mem"),
            split_axis=0,
            concat_axis=0,
            tiled=True,
        ),
        lax.all_to_all(
            send_rank.reshape(group_count, capacity),
            ("clus", "mem"),
            split_axis=0,
            concat_axis=0,
            tiled=True,
        ),
    )
    own_emb = received[0].reshape(slot_count, feature_count)
    own_label = received[1].reshape(slot_count)
    own_rank = received[2].reshape(slot_count)
    other_emb, other_label, other_rank = swapped((own_emb, own_label, own_rank), "sub", 0)
    diag_best, ignored = masked_best(
        own_emb, own_label, own_rank, own_emb, own_label, own_rank, False
    )
    core_side = lax.axis_index("sub")
    is_zero = core_side == 0
    zero_emb = jnp.where(is_zero, own_emb, other_emb)
    zero_label = jnp.where(is_zero, own_label, other_label)
    zero_rank = jnp.where(is_zero, own_rank, other_rank)
    one_emb = jnp.where(is_zero, other_emb, own_emb)
    one_label = jnp.where(is_zero, other_label, own_label)
    one_rank = jnp.where(is_zero, other_rank, own_rank)
    half_count = slot_count // 2
    offset = core_side * half_count
    part_emb = lax.dynamic_slice_in_dim(zero_emb, offset, half_count, 0)
    part_label = lax.dynamic_slice_in_dim(zero_label, offset, half_count, 0)
    part_rank = lax.dynamic_slice_in_dim(zero_rank, offset, half_count, 0)
    half_best, col_part = masked_best(
        part_emb, part_label, part_rank, one_emb, one_label, one_rank, True
    )
    got_half, got_cols = swapped((half_best, col_part), "sub", 0)
    row_side = jnp.concatenate([half_best, got_half])
    cross_best = jnp.where(is_zero, row_side, jnp.maximum(col_part, got_cols))
    nearest = jnp.maximum(diag_best, cross_best)
    returned = lax.all_to_all(
        nearest.reshape(group_count, capacity),
        ("clus", "mem"),
        split_axis=0,
        concat_axis=0,
        tiled=True,
    )
    return returned.reshape(-1)[slot_of]


def local(embeddings, labels, member_rank):
    rows = embeddings.shape[0]
    clus_count, mem_count, sub_count = (lax.axis_size(a) for a in ("clus", "mem", "sub"))
    if fits_kernel(clus_count, mem_count, sub_count, rows):
        return kernel_body(clus_count, mem_count, embeddings, labels, member_rank)
    return body(embeddings, labels, member_rank)


def solution(mesh):
    placed = (
        P(("parts", "clus", "mem", "sub"), None),
        P(("parts", "clus", "mem", "sub")),
        P(("parts", "clus", "mem", "sub")),
    )
    return jax.shard_map(
        local,
        mesh=mesh,
        in_specs=placed,
        out_specs=P(("parts", "clus", "mem", "sub")),
        check_vma=False,
    )
```

```python
import functools
import math

import jax
import jax.numpy as jnp
from jax import lax
from jax.experimental import pallas as pl
from jax.experimental.pallas import tpu as pltpu
from jax.sharding import PartitionSpec as P

CLUS_GROUP = 2
MESH = pl.DeviceIdType.MESH
ROW_TILE = 16
LANES = 128
BYTE = 256
CLASS_STEP = BYTE * BYTE
NO_CAP = 3e38


def flipped(index, mask, size):
    out = 0
    bit = 1
    while bit < size:
        digit = lax.rem(lax.div(index, bit), 2)
        out = out + ((1 - digit) if mask & bit else digit) * bit
        bit *= 2
    return out


def nt_dot(lhs, rhs):
    return lax.dot_general(lhs, rhs, (((1,), (1,)), ((), ())), preferred_element_type=jnp.float32)


def dedup_kernel(
    clus_count,
    mem_count,
    capacity,
    emb_hbm,
    label_hbm,
    rank_hbm,
    out_ref,
    emb,
    label_ref,
    rank_ref,
    caps_own,
    caps_sib,
    send,
    own,
    sib,
    key_out,
    key_in,
    key_own,
    key_sib,
    ret_out,
    ret_in,
    load_sem,
    emb_send,
    emb_recv,
    key_send,
    key_recv,
    fwd_send,
    fwd_recv,
    kf_send,
    kf_recv,
    ret_send,
    ret_recv,
):
    groups = clus_count * mem_count
    rows = emb.shape[0]
    slots = groups * capacity
    tiles = slots // LANES
    per_tile = LANES // capacity
    clus = lax.axis_index("clus")
    mem = lax.axis_index("mem")
    sub = lax.axis_index("sub")
    me = clus * mem_count + mem


    def partner(k):
        return {
            "clus": flipped(clus, k // mem_count, clus_count),
            "mem": flipped(mem, k % mem_count, mem_count),
        }

    sibling = {"sub": 1 - sub}
    load_label = pltpu.make_async_copy(label_hbm, label_ref, load_sem.at[0])
    load_rank = pltpu.make_async_copy(rank_hbm, rank_ref, load_sem.at[1])
    load = pltpu.make_async_copy(emb_hbm, emb, load_sem.at[2])
    load_label.start()
    load.start()
    load_rank.start()
    far_first = list(range(groups - 1, 0, -1))
    barrier = pltpu.get_barrier_semaphore()
    for k in far_first:
        pl.semaphore_signal(barrier, inc=1, device_id=partner(k), device_id_type=MESH)
    pl.semaphore_signal(barrier, inc=1, device_id=sibling, device_id_type=MESH)

    load_label.wait()
    labels = label_ref[...]
    group = lax.div(labels, CLUS_GROUP)
    relative = jnp.bitwise_xor(group, me)
    group_iota = lax.broadcasted_iota(jnp.int32, (groups, rows), 0)
    member = group_iota == relative
    before = lax.broadcasted_iota(jnp.int32, (rows, rows), 0) < lax.broadcasted_iota(
        jnp.int32, (rows, rows), 1
    )
    counts = jnp.dot(
        member.astype(jnp.float32).astype(jnp.bfloat16),
        before.astype(jnp.float32).astype(jnp.bfloat16),
        preferred_element_type=jnp.float32,
    )
    slot = jnp.sum(
        jnp.where(member, counts + (group_iota * capacity).astype(jnp.float32), 0.0),
        axis=0,
        keepdims=True,
    ).astype(jnp.int32)
    place = (
        (lax.broadcasted_iota(jnp.int32, (slots, rows), 0) == slot)
        .astype(jnp.float32)
        .astype(jnp.bfloat16)
    )

    def fill(first, count):
        span = pl.ds(first * capacity, count * capacity)
        send[span, :] = jnp.dot(
            place[first * capacity : (first + count) * capacity],
            emb[...],
            preferred_element_type=jnp.float32,
        ).astype(jnp.bfloat16)

    def send_order(k):
        clus_mask, mem_mask = divmod(k, mem_count)
        near = clus_mask < clus_count // 2
        return near, -clus_mask if near else clus_mask, -mem_mask

    def block(ref, k):
        return ref.at[pl.ds(k * capacity, capacity), :]

    emb_copies, key_copies = {}, {}
    for k in far_first:
        emb_copies[k] = pltpu.make_async_remote_copy(
            src_ref=block(send, k),
            dst_ref=block(own, k),
            send_sem=emb_send.at[k],
            recv_sem=emb_recv.at[k],
            device_id=partner(k),
            device_id_type=MESH,
        )
        key_copies[k] = pltpu.make_async_remote_copy(
            src_ref=key_out.at[k // per_tile],
            dst_ref=key_in.at[k],
            send_sem=key_send.at[k],
            recv_sem=key_recv.at[k],
            device_id=partner(k),
            device_id_type=MESH,
        )
    half = groups // 2
    load_rank.wait()
    ranks = rank_ref[...]
    row_iota = lax.broadcasted_iota(jnp.int32, (8, rows), 0)
    digits = jnp.where(
        row_iota == 0,
        labels - group * CLUS_GROUP + 1,
        jnp.where(
            row_iota == 1,
            lax.div(ranks, BYTE),
            jnp.where(row_iota == 2, lax.rem(ranks, BYTE), 0),
        ),
    )
    placed = nt_dot(digits.astype(jnp.float32).astype(jnp.bfloat16), place)
    keys = placed[0:1] * float(CLASS_STEP) + placed[1:2] * float(BYTE) + placed[2:3]
    for t in range(tiles):
        key_out[t] = keys[:, t * LANES : (t + 1) * LANES]
    load.wait()
    fill(0, groups)
    pl.semaphore_wait(barrier, groups)
    for k in far_first:
        key_copies[k].start()
    for k in sorted(far_first, key=send_order):
        emb_copies[k].start()
    own[pl.ds(0, capacity), :] = send[pl.ds(0, capacity), :]

    forwards = {}
    for k in range(groups):
        forwards[k] = pltpu.make_async_remote_copy(
            src_ref=block(send if k == 0 else own, k),
            dst_ref=block(sib, k),
            send_sem=fwd_send.at[k],
            recv_sem=fwd_recv.at[k],
            device_id=sibling,
            device_id_type=MESH,
        )
    forwards[0].start()
    lane_block = lax.div(lax.broadcasted_iota(jnp.int32, (1, LANES), 1), capacity)
    for k in range(1, groups):
        key_copies[k].wait_recv()
    for t in range(tiles):
        row = jnp.zeros((1, LANES), jnp.float32)
        for k in range(t * per_tile, (t + 1) * per_tile):
            piece = key_out[t] if k == 0 else key_in[k]
            row = jnp.where(lane_block == k % per_tile, piece, row)
        key_own[t] = row
    key_forward = pltpu.make_async_remote_copy(
        src_ref=key_own,
        dst_ref=key_sib,
        send_sem=kf_send,
        recv_sem=kf_recv,
        device_id=sibling,
        device_id_type=MESH,
    )
    key_forward.start()
    row_keys = jnp.concatenate([key_own[t] for t in range(tiles)], axis=1)
    row_base = (
        lax.div(row_keys.astype(jnp.int32), CLASS_STEP) * CLASS_STEP
    ).astype(jnp.float32)
    row_base = jnp.maximum(row_base, 1.0)

    def make_caps(caps, cand_keys):
        for t in range(tiles):
            column = jnp.transpose(jnp.broadcast_to(cand_keys[t], (LANES, LANES)))
            column = jnp.concatenate([column] * tiles, axis=1)
            allowed = (column < row_keys) & (column >= row_base)
            caps[pl.ds(t * LANES, LANES), :] = jnp.where(allowed, NO_CAP, -1.0)

    make_caps(caps_own, key_own)
    key_forward.wait_recv()
    make_caps(caps_sib, key_sib)

    def masked(cands, caps, first, count):
        span = pl.ds(first * capacity, count * capacity)
        scores = jnp.minimum(nt_dot(cands[span, :], own[...]), caps[span, :])
        return jnp.max(scores, axis=0, keepdims=True)

    for k in range(1, groups):
        emb_copies[k].wait_recv()
        forwards[k].start()
    best = jnp.maximum(masked(own, caps_own, 0, groups), -1.0)
    for k in range(groups):
        forwards[k].wait_recv()
    best = jnp.maximum(best, masked(sib, caps_sib, 0, groups))
    for t in range(tiles):
        ret_out[t] = best[:, t * LANES : (t + 1) * LANES]

    returns = {}
    for k in far_first:
        returns[k] = pltpu.make_async_remote_copy(
            src_ref=ret_out.at[k // per_tile],
            dst_ref=ret_in.at[k],
            send_sem=ret_send.at[k],
            recv_sem=ret_recv.at[k],
            device_id=partner(k),
            device_id_type=MESH,
        )
        returns[k].start()
    for k in far_first:
        emb_copies[k].wait_send()
        key_copies[k].wait_send()
    for k in range(groups):
        forwards[k].wait_send()
    key_forward.wait_send()
    for k in range(1, groups):
        returns[k].wait_recv()

    pieces = []
    for t in range(tiles):
        row = jnp.zeros((1, LANES), jnp.float32)
        for k in range(t * per_tile, (t + 1) * per_tile):
            piece = ret_out[t] if k == 0 else ret_in[k]
            row = jnp.where(lane_block == k % per_tile, piece, row)
        pieces.append(row)
    result = jnp.concatenate(pieces, axis=1)
    high = result.astype(jnp.bfloat16).astype(jnp.float32)
    middle = (result - high).astype(jnp.bfloat16).astype(jnp.float32)
    low = result - high - middle
    split_iota = lax.broadcasted_iota(jnp.int32, (8, slots), 0)
    split = jnp.where(
        split_iota == 0,
        high,
        jnp.where(split_iota == 1, middle, jnp.where(split_iota == 2, low, 0.0)),
    ).astype(jnp.bfloat16)
    taken = jnp.dot(split, place, preferred_element_type=jnp.float32)
    out_ref[...] = taken[0:1] + taken[1:2] + taken[2:3]
    for k in far_first:
        returns[k].wait_send()


def kernel_body(clus_count, mem_count, embeddings, labels, member_rank):
    rows, width = embeddings.shape
    groups = clus_count * mem_count
    capacity = 2 * rows // groups
    slots = groups * capacity
    tiles = slots // LANES
    dma = pltpu.SemaphoreType.DMA
    vmem = pl.BlockSpec(memory_space=pltpu.VMEM)
    out = pl.pallas_call(
        functools.partial(dedup_kernel, clus_count, mem_count, capacity),
        out_shape=jax.ShapeDtypeStruct((1, rows), jnp.float32),
        in_specs=[pl.BlockSpec(memory_space=pl.ANY)] * 3,
        out_specs=vmem,
        scratch_shapes=[
            pltpu.VMEM((rows, width), jnp.bfloat16),
            pltpu.VMEM((1, rows), jnp.int32),
            pltpu.VMEM((1, rows), jnp.int32),
            pltpu.VMEM((slots, slots), jnp.float32),
            pltpu.VMEM((slots, slots), jnp.float32),
            pltpu.VMEM((slots, width), jnp.bfloat16),
            pltpu.VMEM((slots, width), jnp.bfloat16),
            pltpu.VMEM((slots, width), jnp.bfloat16),
            pltpu.VMEM((tiles, 1, LANES), jnp.float32),
            pltpu.VMEM((groups, 1, LANES), jnp.float32),
            pltpu.VMEM((tiles, 1, LANES), jnp.float32),
            pltpu.VMEM((tiles, 1, LANES), jnp.float32),
            pltpu.VMEM((tiles, 1, LANES), jnp.float32),
            pltpu.VMEM((groups, 1, LANES), jnp.float32),
            dma((3,)),
            dma((groups,)),
            dma((groups,)),
            dma((groups,)),
            dma((groups,)),
            dma((groups,)),
            dma((groups,)),
            dma,
            dma,
            dma((groups,)),
            dma((groups,)),
        ],
        compiler_params=pltpu.CompilerParams(collective_id=0, has_side_effects=True),
    )(embeddings, labels.reshape(1, rows), member_rank.reshape(1, rows))
    return out.reshape(rows)


def fits_kernel(clus_count, mem_count, sub_count, rows):
    groups = clus_count * mem_count
    capacity = 2 * rows // groups
    return (
        clus_count & (clus_count - 1) == 0
        and mem_count & (mem_count - 1) == 0
        and sub_count == 2
        and groups >= 2
        and rows % LANES == 0
        and capacity % ROW_TILE == 0
        and LANES % capacity == 0
        and rows * groups * sub_count <= CLASS_STEP
    )


def swapped(value, axis, stride):
    mask = 2**stride
    pairs = [(source, source ^ mask) for source in range(lax.axis_size(axis))]
    return lax.ppermute(value, axis, pairs)


def masked_best(row_emb, row_label, row_rank, col_emb, col_label, col_rank, want_columns):
    col_count = col_emb.shape[0]
    block_size = math.gcd(512, col_count)
    block_count = col_count // block_size
    emb_blocks = col_emb.reshape(block_count, block_size, col_emb.shape[1])
    label_blocks = col_label.reshape(block_count, block_size)
    rank_blocks = col_rank.reshape(block_count, block_size)

    def visit_block(running, column_piece):
        piece_emb, piece_label, piece_rank = column_piece
        scores = lax.dot_general(
            row_emb, piece_emb, (((1,), (1,)), ((), ())), preferred_element_type=jnp.float32
        )
        same_cluster = (row_label[:, None] == piece_label[None, :]) & (row_label[:, None] >= 0)
        earlier = piece_rank[None, :] < row_rank[:, None]
        row_best = jnp.max(jnp.where(same_cluster & earlier, scores, jnp.float32(-1.0)), axis=1)
        if want_columns:
            later = same_cluster & jnp.logical_not(earlier)
            col_best = jnp.max(jnp.where(later, scores, jnp.float32(-1.0)), axis=0)
        else:
            col_best = jnp.zeros((0,), jnp.float32)
        return (jnp.maximum(running, row_best), col_best)

    initial = jnp.full((row_emb.shape[0],), -1.0, jnp.float32)
    row_best, col_blocks = lax.scan(visit_block, initial, (emb_blocks, label_blocks, rank_blocks))
    return (row_best, col_blocks.reshape(-1))


def body(embeddings, labels, member_rank):
    row_count = embeddings.shape[0]
    feature_count = embeddings.shape[1]
    clus_count = lax.axis_size("clus")
    mem_count = lax.axis_size("mem")
    group_count = clus_count * mem_count
    capacity = 2 * row_count // group_count
    slot_count = group_count * capacity
    group_of = labels // CLUS_GROUP
    one_hot = (group_of[:, None] == jnp.arange(group_count, dtype=jnp.int32)[None, :]).astype(
        jnp.int32
    )
    running_count = jnp.cumsum(one_hot, axis=0) - 1
    within_group = jnp.sum(one_hot * running_count, axis=1)
    slot_of = group_of * capacity + within_group
    send_emb = jnp.zeros((slot_count, feature_count), jnp.bfloat16).at[slot_of].set(embeddings)
    send_label = jnp.full((slot_count,), -1, jnp.int32).at[slot_of].set(labels)
    send_rank = jnp.zeros((slot_count,), jnp.int32).at[slot_of].set(member_rank)
    received = (
        lax.all_to_all(
            send_emb.reshape(group_count, capacity, feature_count),
            ("clus", "mem"),
            split_axis=0,
            concat_axis=0,
            tiled=True,
        ),
        lax.all_to_all(
            send_label.reshape(group_count, capacity),
            ("clus", "mem"),
            split_axis=0,
            concat_axis=0,
            tiled=True,
        ),
        lax.all_to_all(
            send_rank.reshape(group_count, capacity),
            ("clus", "mem"),
            split_axis=0,
            concat_axis=0,
            tiled=True,
        ),
    )
    own_emb = received[0].reshape(slot_count, feature_count)
    own_label = received[1].reshape(slot_count)
    own_rank = received[2].reshape(slot_count)
    other_emb, other_label, other_rank = swapped((own_emb, own_label, own_rank), "sub", 0)
    diag_best, ignored = masked_best(
        own_emb, own_label, own_rank, own_emb, own_label, own_rank, False
    )
    core_side = lax.axis_index("sub")
    is_zero = core_side == 0
    zero_emb = jnp.where(is_zero, own_emb, other_emb)
    zero_label = jnp.where(is_zero, own_label, other_label)
    zero_rank = jnp.where(is_zero, own_rank, other_rank)
    one_emb = jnp.where(is_zero, other_emb, own_emb)
    one_label = jnp.where(is_zero, other_label, own_label)
    one_rank = jnp.where(is_zero, other_rank, own_rank)
    half_count = slot_count // 2
    offset = core_side * half_count
    part_emb = lax.dynamic_slice_in_dim(zero_emb, offset, half_count, 0)
    part_label = lax.dynamic_slice_in_dim(zero_label, offset, half_count, 0)
    part_rank = lax.dynamic_slice_in_dim(zero_rank, offset, half_count, 0)
    half_best, col_part = masked_best(
        part_emb, part_label, part_rank, one_emb, one_label, one_rank, True
    )
    got_half, got_cols = swapped((half_best, col_part), "sub", 0)
    row_side = jnp.concatenate([half_best, got_half])
    cross_best = jnp.where(is_zero, row_side, jnp.maximum(col_part, got_cols))
    nearest = jnp.maximum(diag_best, cross_best)
    returned = lax.all_to_all(
        nearest.reshape(group_count, capacity),
        ("clus", "mem"),
        split_axis=0,
        concat_axis=0,
        tiled=True,
    )
    return returned.reshape(-1)[slot_of]


def local(embeddings, labels, member_rank):
    rows = embeddings.shape[0]
    clus_count, mem_count, sub_count = (lax.axis_size(a) for a in ("clus", "mem", "sub"))
    if fits_kernel(clus_count, mem_count, sub_count, rows):
        return kernel_body(clus_count, mem_count, embeddings, labels, member_rank)
    return body(embeddings, labels, member_rank)


def solution(mesh):
    placed = (
        P(("parts", "clus", "mem", "sub"), None),
        P(("parts", "clus", "mem", "sub")),
        P(("parts", "clus", "mem", "sub")),
    )
    return jax.shard_map(
        local,
        mesh=mesh,
        in_specs=placed,
        out_specs=P(("parts", "clus", "mem", "sub")),
        check_vma=False,
    )
```
